32 devices in a mesh: seq: 2 (over core), shard: 16 (over z, y, x).
Axes of the slice: x: 2, y: 2, z: 4, core: 2. Of those that a mesh axis runs over, the one named last changes fastest.
Arguments:
- tokens: bfloat16 [16, 2048, 768], P('shard', 'seq'), may hold values from -6 to 6
- lengths: int32 [16, 8], P('shard'), may hold values from 1 to 1024, 2048 in all within a row
- query_weight: bfloat16 [768, 768], P(('seq', 'shard')), may hold values from -0.21875 to 0.21875
- query_bias: bfloat16 [768], P(('seq', 'shard')), may hold values from -3 to 3
- key_weight: bfloat16 [768, 768], P(('seq', 'shard')), may hold values from -0.21875 to 0.21875
- value_weight: bfloat16 [768, 768], P(('seq', 'shard')), may hold values from -0.21875 to 0.21875
- value_bias: bfloat16 [768], P(('seq', 'shard')), may hold values from -3 to 3
- output_weight: bfloat16 [768, 768], P(('seq', 'shard')), may hold values from -1.25 to 1.25
- output_bias: bfloat16 [768], P(('seq', 'shard')), may hold values from -3 to 3
- first_gain: bfloat16 [768], P(('seq', 'shard')), may hold values from 0.5 to 1.5
- first_shift: bfloat16 [768], P(('seq', 'shard')), may hold values from -3 to 3
- up_weight: bfloat16 [768, 3072], P(('seq', 'shard')), may hold values from -0.21875 to 0.21875
- up_bias: bfloat16 [3072], P(('seq', 'shard')), may hold values from -3 to 3
- down_weight: bfloat16 [3072, 768], P(('seq', 'shard')), may hold values from -0.109375 to 0.109375
- down_bias: bfloat16 [768], P(('seq', 'shard')), may hold values from -3 to 3
- second_gain: bfloat16 [768], P(('seq', 'shard')), may hold values from 0.5 to 1.5
- second_shift: bfloat16 [768], P(('seq', 'shard')), may hold values from -3 to 3
- cotangent: bfloat16 [16, 2048, 768], P('shard', 'seq'), may hold values from -6 to 6
Outputs:
- output: bfloat16 [16, 2048, 768], P('shard', 'seq')
- grad_tokens: float32 [16, 2048, 768], P('shard', 'seq')
- grad_query_weight: float32 [768, 768], P(('seq', 'shard'))
- grad_query_bias: float32 [768], P(('seq', 'shard'))
- grad_key_weight: float32 [768, 768], P(('seq', 'shard'))
- grad_value_weight: float32 [768, 768], P(('seq', 'shard'))
- grad_value_bias: float32 [768], P(('seq', 'shard'))
- grad_output_weight: float32 [768, 768], P(('seq', 'shard'))
- grad_output_bias: float32 [768], P(('seq', 'shard'))
- grad_first_gain: float32 [768], P(('seq', 'shard'))
- grad_first_shift: float32 [768], P(('seq', 'shard'))
- grad_up_weight: float32 [768, 3072], P(('seq', 'shard'))
- grad_up_bias: float32 [3072], P(('seq', 'shard'))
- grad_down_weight: float32 [3072, 768], P(('seq', 'shard'))
- grad_down_bias: float32 [768], P(('seq', 'shard'))
- grad_second_gain: float32 [768], P(('seq', 'shard'))
- grad_second_shift: float32 [768], P(('seq', 'shard'))
The draws below stay inside these ranges and needn't reach their ends.
Inputs may be any that keep to these rules, and one draw needn't show every extreme that they name: Each sequence's 8 document lengths add up to 2048, and one of them is exactly 1024.
All inputs are finite; a program needn't handle non-finite values.
Results may differ from the reference program's by a relative error of at most 0.014.
Values may be sent and summed in bfloat16 or wider, within the bound.
No kernel may reach another device: no remote copies, remote signals or barrier semaphores. Data moves between devices by JAX's collectives and lax.ppermute only.
A program may use at most 192 MiB of HBM per device.

```python
import math
import jax
import jax.numpy as jnp
import numpy as np
from jax import lax

D = 768
HEADS = 12
HEAD_DIM = 64
FF = 3072
LEN = 2048
DOCS = 8
MOST = 1024
SEQS = 16


def strengthened(array, own_key, source, target, parts, factor):
    owner, partner = [(jnp.arange(array.shape[position]) // (array.shape[position] // parts)).reshape([-1 if axis == position else 1 for axis in range(array.ndim)]) for position in (source, target)]
    chosen = jax.random.permutation(own_key, parts)[partner]
    strong = (owner == chosen) | (owner == (partner + parts // 2) % parts)
    return jnp.where(strong, factor * array, array)


def block_levels(stream_key, shape, cuts, low, high):
    factor_of, own = 1.0, jax.random.fold_in(stream_key, 6)
    for dim, shards_of in cuts:
        heights = jnp.exp(jax.random.uniform(jax.random.fold_in(own, dim), (shards_of,), jnp.float32, low / len(cuts), high / len(cuts)))
        factor_of = factor_of * jnp.repeat(heights, shape[dim] // shards_of).reshape([-1 if axis == dim else 1 for axis in range(len(shape))])
    return factor_of


def length_profile(count, total, bound, skew):
    loads = [(1 << 20) // math.isqrt(grade ** skew) + 1 for grade in range(2, count + 1)]
    rest, given = total - bound - (count - 1), [1] * (count - 1)
    while rest > 0:
        candidates = [i for i in range(count - 1) if given[i] < bound]
        mass, budget = sum([loads[i] for i in candidates]), rest
        for i in candidates:
            more = min(bound - given[i], max(1, budget * loads[i] // mass), rest)
            given[i] = given[i] + more
            rest = rest - more
    return np.array([bound] + given)


def ragged_sizes(key, count, total, most, skew):
    if count == 2:
        one = jax.random.randint(key, (), max(1, total - most), min(most, total - 1) + 1)
        return jnp.stack([one, total - one])
    sizes = jnp.asarray(length_profile(count, total, most, skew), jnp.int32)
    pairs = (count - 1) // 2
    giver, taker = sizes[1:1 + 2 * pairs:2], sizes[2:2 + 2 * pairs:2]
    room = jnp.minimum(giver - 1, most - taker)
    passed = jax.random.randint(jax.random.fold_in(key, 1), (pairs,), 0, 1 << 20) % (room + 1)
    sizes = sizes.at[1:1 + 2 * pairs:2].set(giver - passed).at[2:2 + 2 * pairs:2].set(taker + passed)
    return sizes[jax.random.permutation(jax.random.fold_in(key, 2), count)]


def bell_draw(rng, dims, width, bound, cuts=(), kind=jnp.bfloat16):
    values = width * jax.random.normal(rng, dims, jnp.float32)
    if cuts:
        values = values * block_levels(rng, dims, cuts, -0.22, 0.18)
    return jnp.clip(values, -bound, bound).astype(kind)


def bell_draw_with(stream_key, extent, width, reach, split, heavy, held_as=jnp.bfloat16):
    drawn = width * jax.random.normal(stream_key, extent, jnp.float32)
    if split:
        drawn = drawn * block_levels(stream_key, extent, split, -0.22, 0.18)
    return jnp.clip(strengthened(drawn, jax.random.fold_in(stream_key, 3), *heavy), -reach, reach).astype(held_as)


def setup_inputs(seed: int = 0) -> dict:
    key_of = jax.random.split(jax.random.key(seed), 19)
    return {
        "tokens": bell_draw_with(key_of[0], (SEQS, LEN, D), 1.0, 6.0, ((0, 16), (1, 2)), (0, 2, 16, 2.0)),
        "lengths": jax.vmap(lambda own: ragged_sizes(own, DOCS, LEN, MOST, 2))(jax.random.split(key_of[1], SEQS)).reshape((SEQS, DOCS)).astype(jnp.int32),
        "query_weight": bell_draw(key_of[2], (D, D), D ** -0.5, 0.21875, ((0, 32),)),
        "query_bias": bell_draw(key_of[3], (D,), 0.5, 3.0, ((0, 32),)),
        "key_weight": bell_draw(key_of[4], (D, D), D ** -0.5, 0.21875, ((0, 32),)),
        "value_weight": bell_draw(key_of[5], (D, D), D ** -0.5, 0.21875, ((0, 32),)),
        "value_bias": bell_draw(key_of[6], (D,), 0.5, 3.0, ((0, 32),)),
        "output_weight": bell_draw(key_of[7], (D, D), (D // 32) ** -0.5, 1.25, ((0, 32),)),
        "output_bias": bell_draw(key_of[8], (D,), 0.5, 3.0, ((0, 32),)),
        "first_gain": jnp.clip(1.0 + 0.1 * jax.random.normal(key_of[9], (D,), jnp.float32), 0.5, 1.5).astype(jnp.bfloat16),
        "first_shift": bell_draw(key_of[10], (D,), 0.5, 3.0, ((0, 32),)),
        "up_weight": bell_draw(key_of[11], (D, FF), D ** -0.5, 0.21875, ((0, 32),)),
        "up_bias": bell_draw(key_of[12], (FF,), 0.5, 3.0, ((0, 32),)),
        "down_weight": bell_draw(key_of[13], (FF, D), FF ** -0.5, 0.109375, ((0, 32),)),
        "down_bias": bell_draw(key_of[14], (D,), 0.5, 3.0, ((0, 32),)),
        "second_gain": jnp.clip(1.0 + 0.1 * jax.random.normal(key_of[15], (D,), jnp.float32), 0.5, 1.5).astype(jnp.bfloat16),
        "second_shift": bell_draw(key_of[16], (D,), 0.5, 3.0, ((0, 32),)),
        "cotangent": bell_draw(key_of[17], (SEQS, LEN, D), 1.0, 6.0, ((0, 16), (1, 2))),
    }


@jax.custom_vjp
def low(v):
    return lax.optimization_barrier(v.astype(jnp.bfloat16)).astype(jnp.float32)

@jax.custom_vjp
def low_back(v):
    return v

def low_keep(v):
    return (low(v), None)

def low_pass(kept, grad):
    return (grad,)

def back_keep(v):
    return (v, None)

def back_low(kept, grad):
    return (low(grad),)
low.defvjp(low_keep, low_pass)
low_back.defvjp(back_keep, back_low)

def product(left, right):
    return jnp.dot(left, right, precision=lax.Precision.HIGHEST)

def layer_norm(hidden, gain, shift):
    centred = hidden - lax.optimization_barrier(jnp.mean(hidden, axis=-1, keepdims=True))
    normed = centred * lax.rsqrt(lax.optimization_barrier(jnp.mean(centred * centred, axis=-1, keepdims=True)) + 1e-12)
    return normed * gain + shift

def doc_index(lengths_row, count):
    ends = jnp.cumsum(lengths_row)
    places = jnp.arange(count, dtype=jnp.int32)
    return lax.optimization_barrier(jnp.sum((places[:, None] >= ends[None, :]).astype(jnp.int32), axis=1))

def layer_seq(params, inputs, lengths_row):
    w_query, b_query, w_key, w_value, b_value, w_out, b_out, gain_one, shift_one, w_up, b_up, w_down, b_down, gain_two, shift_two = params
    count = inputs.shape[0]
    query = low(low_back(product(inputs, w_query) + b_query)).reshape(count, HEADS, HEAD_DIM)
    keys = low(low_back(product(inputs, w_key))).reshape(count, HEADS, HEAD_DIM)
    values = low(low_back(product(inputs, w_value) + b_value)).reshape(count, HEADS, HEAD_DIM)
    doc = doc_index(lengths_row, count)
    same = doc[:, None] == doc[None, :]
    scores = jnp.einsum('qhd,khd->hqk', query, keys, precision=lax.Precision.HIGHEST) * HEAD_DIM ** (-0.5)
    scores = low_back(jnp.where(same[None], scores, -1e+30))
    peak = lax.optimization_barrier(jnp.max(scores, axis=-1, keepdims=True))
    log_sum = peak + jnp.log(lax.optimization_barrier(jnp.sum(jnp.exp(scores - peak), axis=-1, keepdims=True)))
    attn_prob = jnp.exp(scores - log_sum)
    mixed = jnp.einsum('hqk,khd->qhd', low(attn_prob), values, precision=lax.Precision.HIGHEST).reshape(count, D)
    mixed = low(low_back(mixed))
    branch = low_back(product(mixed, w_out) + b_out)
    first = layer_norm(inputs + branch, gain_one, shift_one)
    preact = low_back(product(low(first), w_up) + b_up)
    activated = low(jax.nn.gelu(preact, approximate=False))
    second_in = first + low_back(product(activated, w_down) + b_down)
    return layer_norm(second_in, gain_two, shift_two)

def reference(tokens, lengths, query_weight, query_bias, key_weight, value_weight, value_bias, output_weight, output_bias, first_gain, first_shift, up_weight, up_bias, down_weight, down_bias, second_gain, second_shift, cotangent):
    params = tuple((item.astype(jnp.float32) for item in (query_weight, query_bias, key_weight, value_weight, value_bias, output_weight, output_bias, first_gain, first_shift, up_weight, up_bias, down_weight, down_bias, second_gain, second_shift)))
    inputs = tokens.astype(jnp.float32)

    def forward(weights, data):

        def one_seq(pair):
            return layer_seq(weights, pair[0], pair[1])
        return lax.map(jax.checkpoint(one_seq), (data, lengths))
    result, pullback = jax.vjp(forward, params, inputs)
    grads, grad_inputs = pullback(cotangent.astype(jnp.float32))
    return (result.astype(jnp.bfloat16), grad_inputs, grads[0], grads[1], grads[2], grads[3], grads[4], grads[5], grads[6], grads[7], grads[8], grads[9], grads[10], grads[11], grads[12], grads[13], grads[14])
```

```python
import jax
import jax.numpy as jnp
from jax import lax
from jax.experimental import pallas as pl
from jax.experimental.pallas import tpu as pltpu
from jax.sharding import PartitionSpec as P

HEADS = 12
HEAD_DIM = 64
BLOCK = 256
LOW = 4
BF16 = jnp.bfloat16
F32 = jnp.float32
MASKED = -1e30


def dot(left, right, dims):
    return lax.dot_general(left, right, (dims, ((), ())), preferred_element_type=F32)


def nn(left, right):
    return dot(left, right, ((1,), (0,)))


def nt(left, right):
    return dot(left, right, ((1,), (1,)))


def tn(left, right):
    return dot(left, right, ((0,), (0,)))


def doc_tables(lengths, count):
    ends = jnp.cumsum(lengths)
    starts = ends - lengths
    docs = lengths.shape[0]
    place = jnp.arange(count, dtype=jnp.int32)
    inside = (place[:, None] >= starts[None, :]) & (place[:, None] < ends[None, :])
    inside_t = (place[None, :] >= starts[:, None]) & (place[None, :] < ends[:, None])
    query_rows = jnp.pad(inside_t.astype(BF16), ((0, HEAD_DIM - docs), (0, 0)))
    penalty = jnp.where(inside, 0.0, MASKED).astype(BF16)
    half = jnp.concatenate(
        [penalty, jnp.ones((count, 3), BF16), jnp.zeros((count, HEAD_DIM - docs - 3), BF16)], 1
    )
    key_cols = jnp.concatenate([half, half], 1)
    first = jnp.arange(count // BLOCK, dtype=jnp.int32) * BLOCK
    last = first + BLOCK - 1
    begin = jnp.max(jnp.where(starts[None, :] <= first[:, None], starts[None, :], 0), 1)
    end = jnp.min(jnp.where(ends[None, :] > last[:, None], ends[None, :], count), 1)
    return (
        (begin // BLOCK).astype(jnp.int32),
        ((end + BLOCK - 1) // BLOCK).astype(jnp.int32),
        query_rows,
        key_cols,
    )


def join(part, extra, head):
    return jnp.concatenate([part, extra] if head % 2 == 0 else [extra, part], 0)


def fill_pairs(out, source, extra_of, count, heads):
    def step(index, _):
        rows = pl.ds(pl.multiple_of(index * BLOCK, BLOCK), BLOCK)
        lane = lax.broadcasted_iota(jnp.int32, (BLOCK, 128), 1)
        extra = extra_of(rows)
        for head in range(0, heads, 2):
            pair = source[rows, 64 * head : 64 * head + 128]
            out[head, rows] = jnp.where(lane < 64, pair, extra)
            out[head + 1, rows] = jnp.where(lane < 64, extra, pair)
        return 0

    lax.fori_loop(0, count // BLOCK, step, 0)


def attend_kernel(
    lo, hi, query_t, keys, values_t, query_rows, key_cols, out_t, log_sum, keys_ext, total_t, stats
):
    count = keys.shape[0]
    heads = query_t.shape[0] // HEAD_DIM
    block = pl.program_id(0)

    @pl.when(block == 0)
    def _():
        fill_pairs(keys_ext, keys, lambda rows: key_cols[rows, :], count, heads)

    extra = query_rows[...]
    query_ext = [join(query_t[64 * h : 64 * h + 64, :], extra, h) for h in range(heads)]
    total_t[...] = jnp.zeros_like(total_t)
    stats[0] = jnp.full(stats.shape[1:], MASKED, F32)
    stats[1] = jnp.zeros(stats.shape[1:], F32)

    def step(index, _):
        rows = pl.ds(pl.multiple_of(index * BLOCK, BLOCK), BLOCK)
        scores = [nn(keys_ext[h, rows, :], query_ext[h]) for h in range(heads)]
        for h in range(heads):
            top = stats[0, h : h + 1, :]
            new_top = jnp.maximum(top, jnp.max(scores[h], axis=0, keepdims=True))
            prob = jnp.exp(scores[h] - new_top)
            keep = jnp.exp(top - new_top)
            stats[1, h : h + 1, :] = stats[1, h : h + 1, :] * keep + jnp.sum(
                prob, axis=0, keepdims=True
            )
            stats[0, h : h + 1, :] = new_top
            total_t[h] = total_t[h] * keep + nn(
                values_t[64 * h : 64 * h + 64, rows], prob.astype(BF16)
            )
        return 0

    lax.fori_loop(lo[block], hi[block], step, 0)
    for h in range(heads):
        norm = stats[1, h : h + 1, :]
        out_t[64 * h : 64 * h + 64, :] = total_t[h] * (1.0 / norm)
        log_sum[h : h + 1, :] = stats[0, h : h + 1, :] + jnp.log(norm)


def attend(lo, hi, query_t, keys, values_t, query_rows, key_cols):
    count, width = keys.shape
    heads = width // HEAD_DIM
    whole = lambda shape: pl.BlockSpec(shape, lambda b, *_: (0, 0))
    column = lambda rows: pl.BlockSpec((rows, BLOCK), lambda b, *_: (0, b))
    return pl.pallas_call(
        attend_kernel,
        grid_spec=pltpu.PrefetchScalarGridSpec(
            num_scalar_prefetch=2,
            grid=(count // BLOCK,),
            in_specs=[
                column(width),
                whole((count, width)),
                whole((width, count)),
                column(HEAD_DIM),
                whole((count, 128)),
            ],
            out_specs=[column(width), column(8)],
            scratch_shapes=[
                pltpu.VMEM((heads, count, 128), BF16),
                pltpu.VMEM((heads, HEAD_DIM, BLOCK), F32),
                pltpu.VMEM((2, 8, BLOCK), F32),
            ],
        ),
        out_shape=[
            jax.ShapeDtypeStruct((width, count), F32),
            jax.ShapeDtypeStruct((8, count), F32),
        ],
        name="attend",
        cost_estimate=pl.CostEstimate(
            flops=4 * count * count * width, bytes_accessed=12 * count * width, transcendentals=0
        ),
    )(lo, hi, query_t, keys, values_t, query_rows, key_cols)


def three_parts(value):
    high = value.astype(BF16).astype(F32)
    middle = (value - high).astype(BF16).astype(F32)
    return (high, middle, value - high - middle)


def attend_back_kernel(
    lo, hi, query_t, keys, values, grad, out_t, log_sum, query_rows, key_cols,
    grad_all, keys_ext, values_ext, keys_t, grad_keys, grad_values,
):
    count, width = keys.shape
    heads = width // HEAD_DIM
    block = pl.program_id(0)

    @pl.when(block == 0)
    def _():
        fill_pairs(keys_ext, keys, lambda rows: key_cols[rows, :], count, heads)
        fill_pairs(values_ext, values, lambda rows: jnp.ones((BLOCK, 128), BF16), count, heads)

        def turn(index, _):
            rows = pl.ds(pl.multiple_of(index * BLOCK, BLOCK), BLOCK)
            keys_t[:, rows] = keys[rows, :].T
            return 0

        lax.fori_loop(0, count // BLOCK, turn, 0)
        grad_keys[...] = jnp.zeros_like(grad_keys)
        grad_values[...] = jnp.zeros_like(grad_values)

    row = lax.broadcasted_iota(jnp.int32, (HEAD_DIM, BLOCK), 0)
    extra = query_rows[...].astype(F32)
    grad_blk = grad[...]
    grad_t = grad_blk.T
    query_blk = query_t[...].T
    query_ext, grad_ext, query_own, grad_own = [], [], [], []
    for h in range(heads):
        span = slice(64 * h, 64 * h + 64)
        a, b, c = three_parts(-log_sum[h : h + 1, :])
        rows = jnp.where(row == 8, a, jnp.where(row == 9, b, jnp.where(row == 10, c, extra)))
        query_ext.append(join(query_t[span, :], rows.astype(BF16), h))
        delta = jnp.sum(grad_t[span, :].astype(F32) * out_t[span, :], axis=0, keepdims=True)
        a, b, c = three_parts(-delta)
        rows = jnp.where(row == 0, a, jnp.where(row == 1, b, jnp.where(row == 2, c, 0.0)))
        grad_ext.append(join(grad_t[span, :], rows.astype(BF16), h))
        query_own.append(query_blk[:, span])
        grad_own.append(grad_blk[:, span])

    def step(index, carry):
        rows = pl.ds(pl.multiple_of(index * BLOCK, BLOCK), BLOCK)
        scores = [nn(keys_ext[h, rows, :], query_ext[h]) for h in range(heads)]
        lifts = [nn(values_ext[h, rows, :], grad_ext[h]) for h in range(heads)]
        out = []
        for h in range(heads):
            prob = jnp.exp(scores[h])
            grad_scores = (prob * lifts[h]).astype(BF16)
            grad_values[h, rows, :] += nn(prob.astype(BF16), grad_own[h])
            grad_keys[h, rows, :] += nn(grad_scores, query_own[h])
            out.append(carry[h] + nn(keys_t[64 * h : 64 * h + 64, rows], grad_scores))
        return tuple(out)

    zero = jnp.zeros((HEAD_DIM, BLOCK), F32)
    grads = lax.fori_loop(lo[block], hi[block], step, (zero,) * heads)
    own = pl.ds(pl.multiple_of(block * BLOCK, BLOCK), BLOCK)
    for h in range(0, heads, 2):
        pair = jnp.concatenate([grads[h], grads[h + 1]], 0) * (HEAD_DIM**-0.5)
        grad_all[own, 64 * h : 64 * h + 128] = pair.T.astype(BF16)

    @pl.when(block == pl.num_programs(0) - 1)
    def _():
        def finish(index, _):
            rows = pl.ds(pl.multiple_of(index * BLOCK, BLOCK), BLOCK)
            for h in range(0, heads, 2):
                for place, held in ((width, grad_keys), (2 * width, grad_values)):
                    pair = jnp.concatenate([held[h, rows, :], held[h + 1, rows, :]], 1)
                    grad_all[rows, place + 64 * h : place + 64 * h + 128] = pair.astype(BF16)
            return 0

        lax.fori_loop(0, count // BLOCK, finish, 0)


def attend_back(lo, hi, query_t, keys, values, grad, out_t, log_sum, query_rows, key_cols):
    count, width = keys.shape
    heads = width // HEAD_DIM
    whole = lambda shape: pl.BlockSpec(shape, lambda b, *_: (0, 0))
    column = lambda rows: pl.BlockSpec((rows, BLOCK), lambda b, *_: (0, b))
    return pl.pallas_call(
        attend_back_kernel,
        grid_spec=pltpu.PrefetchScalarGridSpec(
            num_scalar_prefetch=2,
            grid=(count // BLOCK,),
            in_specs=[
                column(width),
                whole((count, width)),
                whole((count, width)),
                pl.BlockSpec((BLOCK, width), lambda b, *_: (b, 0)),
                column(width),
                column(8),
                column(HEAD_DIM),
                whole((count, 128)),
            ],
            out_specs=whole((count, 3 * width)),
            scratch_shapes=[
                pltpu.VMEM((heads, count, 128), BF16),
                pltpu.VMEM((heads, count, 128), BF16),
                pltpu.VMEM((width, count), BF16),
                pltpu.VMEM((heads, count, HEAD_DIM), F32),
                pltpu.VMEM((heads, count, HEAD_DIM), F32),
            ],
        ),
        out_shape=jax.ShapeDtypeStruct((count, 3 * width), BF16),
        name="attend_back",
        cost_estimate=pl.CostEstimate(
            flops=10 * count * count * width, bytes_accessed=20 * count * width, transcendentals=0
        ),
    )(lo, hi, query_t, keys, values, grad, out_t, log_sum, query_rows, key_cols)


def swap(array):
    return lax.ppermute(array, "seq", [(0, 1), (1, 0)])


def low_hop(array, mask):
    size = lax.axis_size("shard")
    return lax.ppermute(
        array, "shard", [(a, a // LOW * LOW + ((a % LOW) ^ mask)) for a in range(size)]
    )


def high_hop(array, step):
    size = lax.axis_size("shard")
    return lax.ppermute(
        array,
        "shard",
        [(a, (a // LOW + step) % (size // LOW) * LOW + a % LOW) for a in range(size)],
    )


def put(whole, part, index):
    return lax.dynamic_update_slice_in_dim(whole, part[None], index, 0)


def pick(whole, index, axis=0):
    return lax.dynamic_index_in_dim(whole, index, axis, keepdims=False)


def gather_shards(block):
    high = lax.axis_size("shard") // LOW
    index = lax.axis_index("shard")
    mine_high, mine_low = index // LOW, index % LOW
    column = put(jnp.zeros((high, *block.shape), block.dtype), block, mine_high)
    for step in range(1, high):
        column = put(column, high_hop(block, step), (mine_high - step) % high)
    whole = put(jnp.zeros((LOW, *column.shape), block.dtype), column, mine_low)
    for mask in range(1, LOW):
        whole = put(whole, low_hop(column, mask), mine_low ^ mask)
    return whole


def scatter_low(take, mine_low):
    received = [low_hop(take(mine_low ^ mask), mask) for mask in range(1, LOW)]
    total = take(mine_low).astype(F32)
    for part in received:
        total = total + part.astype(F32)
    return total


def scatter_high(column):
    high = column.shape[0]
    mine = lax.axis_index("shard") // LOW
    low = column.astype(BF16)
    received = [high_hop(pick(low, (mine + step) % high), step) for step in range(1, high)]
    total = pick(column, mine)
    for part in received:
        total = total + part.astype(F32)
    return total


def norm(hidden):
    centred = hidden - jnp.mean(hidden, axis=-1, keepdims=True)
    factor = lax.rsqrt(jnp.mean(centred * centred, axis=-1, keepdims=True) + 1e-12)
    return (centred * factor, factor)


def norm_back(grad, normed, factor, gain):
    scaled = grad * gain
    inner = (
        scaled
        - jnp.mean(scaled, axis=-1, keepdims=True)
        - normed * jnp.mean(scaled * normed, axis=-1, keepdims=True)
    )
    return factor * inner


def on_device(
    tokens, lengths, query_weight, query_bias, key_weight, value_weight, value_bias,
    output_weight, output_bias, first_gain, first_shift, up_weight, up_bias, down_weight,
    down_bias, second_gain, second_shift, cotangent,
):
    _, half_len, width = tokens.shape
    count = 2 * half_len
    half = width // 2
    hidden = up_weight.shape[1]
    rows = query_weight.shape[0]
    wide = hidden // width
    shards = lax.axis_size("shard")
    high = shards // LOW
    devices = 2 * shards
    me = lax.axis_index("seq")
    index = lax.axis_index("shard")
    mine_low = index % LOW
    own_tokens = tokens[0]

    both = jnp.concatenate([query_weight, key_weight, value_weight], 0).reshape(3, rows, 2, half)
    kept = pick(both, me, 2)
    got = swap(pick(both, 1 - me, 2))
    pair = put(put(jnp.zeros((2, 3, rows, half), BF16), kept, me), got, 1 - me)
    small = jnp.concatenate([query_bias, value_bias])
    small = jnp.pad(small, (0, half - small.shape[0])).reshape(1, 1, 1, half)
    block = jnp.concatenate(
        [pair.reshape(1, 1, 6 * rows, half), jnp.pad(small, ((0, 0), (0, 0), (0, 7), (0, 0)))], 2
    )[0, 0]
    gathered = gather_shards(block)
    weights = gathered[:, :, : 6 * rows].reshape(LOW, high, 2, 3, rows, half)
    weights = weights.transpose(3, 2, 1, 0, 4, 5).reshape(3, width, half)
    w_query, w_key, w_value = weights[0], weights[1], weights[2]
    biases = gathered[:, :, 6 * rows, : 2 * rows].reshape(LOW, high, 2, rows)
    biases = biases.transpose(2, 1, 0, 3).reshape(2, half).astype(F32)
    b_query, b_value = biases[0], biases[1]

    vectors = jnp.concatenate(
        [output_bias, first_gain, first_shift, down_bias, second_gain, second_shift, up_bias]
    )
    line = jnp.pad(vectors, (0, width - vectors.shape[0])).reshape(1, width)
    pack = jnp.concatenate(
        [
            output_weight,
            up_weight.reshape(rows, wide, width).transpose(1, 0, 2).reshape(wide * rows, width),
            down_weight,
            jnp.pad(line, ((0, 7), (0, 0))),
        ],
        0,
    )
    rest = lax.all_gather(pack, ("seq", "shard"), axis=0, tiled=False)

    other_tokens = swap(own_tokens)
    both_tokens = put(put(jnp.zeros((2, half_len, width), BF16), own_tokens, me), other_tokens, 1 - me)
    x = both_tokens.reshape(count, width)

    scale = HEAD_DIM**-0.5
    query_t = (
        (dot(w_query, x, ((0,), (1,))) + b_query[:, None]).astype(BF16) * jnp.asarray(scale, BF16)
    )
    keys = nn(x, w_key).astype(BF16)
    values_t = (dot(w_value, x, ((0,), (1,))) + b_value[:, None]).astype(BF16)
    values = (nn(x, w_value) + b_value).astype(BF16)

    lo, hi, query_rows, key_cols = doc_tables(lengths[0], count)
    out_t, log_sum = attend(lo, hi, query_t, keys, values_t, query_rows, key_cols)
    low_t = out_t.astype(BF16).reshape(half, 2, half_len)
    mixed_t = put(
        put(jnp.zeros((2, half, half_len), BF16), pick(low_t, me, 1), me),
        swap(pick(low_t, 1 - me, 1)),
        1 - me,
    ).reshape(width, half_len)

    w_out = rest[:, :rows].reshape(width, width)
    w_up = (
        rest[:, rows : rows + wide * rows]
        .reshape(devices, wide, rows, width)
        .transpose(0, 2, 1, 3)
        .reshape(width, hidden)
    )
    w_down = rest[:, rows + wide * rows : rows + 2 * wide * rows].reshape(hidden, width)
    lines = rest[:, rows + 2 * wide * rows]
    b_out, gain_one, shift_one, b_down, gain_two, shift_two = (
        lines[:, : 6 * rows].reshape(devices, 6, rows).transpose(1, 0, 2).reshape(6, width).astype(F32)
    )
    b_up = lines[:, 6 * rows : 6 * rows + wide * rows].reshape(hidden).astype(F32)

    branch = tn(mixed_t, w_out) + b_out
    normed_one, factor_one = norm(own_tokens.astype(F32) + branch)
    first = normed_one * gain_one + shift_one
    first_low = first.astype(BF16)
    preact = nn(first_low, w_up) + b_up
    cdf = 0.5 * (1.0 + lax.erf(preact * (0.5**0.5)))
    density = jnp.exp(-0.5 * preact * preact) * 0.3989422804014327
    activated = (preact * cdf).astype(BF16)
    slope = (cdf + preact * density).astype(BF16)
    second_in = first + nn(activated, w_down) + b_down
    normed_two, factor_two = norm(second_in)
    output = (normed_two * gain_two + shift_two).astype(BF16)

    grad_y = cotangent[0].astype(F32)
    d_gain_two = jnp.sum(grad_y * normed_two, axis=0)
    d_shift_two = jnp.sum(grad_y, axis=0)
    g_second = norm_back(grad_y, normed_two, factor_two, gain_two)
    g_down = g_second.astype(BF16)
    d_down = tn(activated, g_down).astype(BF16)
    d_b_down = jnp.sum(g_down.astype(F32), axis=0)
    g_pre = (nt(g_down, w_down) * slope.astype(F32)).astype(BF16)
    d_up = tn(first_low, g_pre).astype(BF16)
    d_b_up = jnp.sum(g_pre.astype(F32), axis=0)
    g_first = g_second + nt(g_pre, w_up)
    d_gain_one = jnp.sum(g_first * normed_one, axis=0)
    d_shift_one = jnp.sum(g_first, axis=0)
    g_res = norm_back(g_first, normed_one, factor_one, gain_one)
    g_branch = g_res.astype(BF16)
    d_out = nn(mixed_t, g_branch).astype(BF16)
    d_b_out = jnp.sum(g_branch.astype(F32), axis=0)
    g_mixed = nt(g_branch, w_out).astype(BF16).reshape(half_len, 2, half)
    grad_heads = put(
        put(jnp.zeros((2, half_len, half), BF16), pick(g_mixed, me, 1), me),
        swap(pick(g_mixed, 1 - me, 1)),
        1 - me,
    ).reshape(count, half)

    parts = [
        d_out.reshape(2, high, LOW, 1, rows, width),
        d_up.reshape(2, high, LOW, rows, wide, width).transpose(0, 1, 2, 4, 3, 5),
        d_down.reshape(2, high, LOW, wide, rows, width),
    ]
    grads = jnp.stack([d_b_out, d_gain_one, d_shift_one, d_b_down, d_gain_two, d_shift_two])
    grads = grads.reshape(6, devices, rows).transpose(1, 0, 2).reshape(devices, 6 * rows)
    grads = jnp.concatenate([grads, d_b_up.reshape(devices, wide * rows)], 1)
    grads = jnp.pad(grads, ((0, 0), (0, width - grads.shape[1]))).astype(BF16)
    grads = jnp.pad(grads.reshape(2, high, LOW, 1, 1, width), ((0, 0),) * 4 + ((0, rows - 1), (0, 0)))
    packed = jnp.concatenate([*parts, grads], 3)
    chip = pick(packed, me).astype(F32) + swap(pick(packed, 1 - me)).astype(F32)
    chip = chip.astype(BF16)
    column = scatter_low(lambda low: pick(chip, low, 1), mine_low)
    owned = scatter_high(column)

    grad_qkv = attend_back(
        lo, hi, query_t, keys, values, grad_heads, out_t, log_sum, query_rows, key_cols
    )
    d_qkv = tn(x, grad_qkv)
    d_bias = jnp.sum(grad_qkv.astype(F32), axis=0)
    d_bias = jnp.stack([d_bias[:half], d_bias[2 * half :]])

    terms = d_qkv.astype(BF16).reshape(2, high, LOW, rows, 3 * half)
    lines = d_bias.reshape(2, high, LOW, rows).transpose(1, 2, 0, 3).reshape(high, LOW, 2 * rows)
    lines = jnp.pad(lines, ((0, 0), (0, 0), (0, 3 * half - 2 * rows))).astype(BF16)
    lines = jnp.pad(lines.reshape(high, LOW, 1, 3 * half), ((0, 0), (0, 0), (0, 7), (0, 0)))
    terms = jnp.concatenate(
        [terms.transpose(1, 2, 0, 3, 4).reshape(high, LOW, 2 * rows, 3 * half), lines], 2
    )
    own_qkv = scatter_high(scatter_low(lambda low: pick(terms, low, 1), mine_low))
    r_biases = own_qkv[2 * rows, : 2 * rows].reshape(2, rows)
    two = own_qkv[: 2 * rows].reshape(2, rows, 3, half)
    mine, theirs = pick(two, me), swap(pick(two, 1 - me))
    r_qkv = put(put(jnp.zeros((2, rows, 3, half), F32), mine, me), theirs, 1 - me)
    r_qkv = r_qkv.transpose(2, 1, 0, 3).reshape(3, rows, width)

    w_all = jnp.concatenate([w_query, w_key, w_value], 1)
    back = nt(grad_qkv, w_all).reshape(2, half_len, width)
    grad_tokens = g_res + pick(back, me) + swap(pick(back, 1 - me))

    r_out = owned[0]
    r_up = owned[1 : 1 + wide].transpose(1, 0, 2).reshape(rows, hidden)
    r_down = owned[1 + wide : 1 + 2 * wide].reshape(wide * rows, width)
    r_line = owned[1 + 2 * wide, 0]
    r_vec = r_line[: 6 * rows].reshape(6, rows)
    r_b_up = r_line[6 * rows : 6 * rows + wide * rows]
    return (
        output[None], grad_tokens[None],
        r_qkv[0], r_biases[0], r_qkv[1], r_qkv[2], r_biases[1],
        r_out, r_vec[0], r_vec[1], r_vec[2], r_up, r_b_up, r_down, r_vec[3], r_vec[4], r_vec[5],
    )


def solution(mesh):
    rows = P(("seq", "shard"), None)
    line = P(("seq", "shard"))
    data = P("shard", "seq", None)
    return jax.shard_map(
        on_device,
        mesh=mesh,
        in_specs=(
            data, P("shard", None), rows, line, rows, rows, line, rows, line, line, line,
            rows, line, rows, line, line, line, data,
        ),
        out_specs=(
            data, data, rows, line, rows, rows, line, rows, line, line, line, rows, line, rows,
            line, line, line,
        ),
        check_vma=False,
    )
```
